256 devices in a mesh: pipe: 4 (over x), dp: 64 (over z, y, core).
Axes of the slice: x: 4, y: 4, z: 8, core: 2. Of those that a mesh axis runs over, the one named last changes fastest.
Arguments:
- hidden: bfloat16 [4, 2048, 3072], P(None, 'dp'), may hold values from -6 to 6
- w_query: bfloat16 [4, 2, 3072, 1536], P('pipe', None, 'dp'), may hold values from -0.109375 to 0.109375
- w_key: bfloat16 [4, 2, 3072, 1536], P('pipe', None, 'dp'), may hold values from -0.109375 to 0.109375
- w_value: bfloat16 [4, 2, 3072, 1536], P('pipe', None, 'dp'), may hold values from -0.109375 to 0.109375
- w_out: bfloat16 [4, 2, 1536, 3072], P('pipe', None, None, 'dp'), may hold values from -0.15625 to 0.15625
- video_len: int32 [4, 16], replicated, may hold values from 1 to 96
- audio_len: int32 [4, 16], replicated, may hold values from 1 to 32
Outputs:
- final: bfloat16 [4, 2048, 3072], P('pipe', 'dp')
The draws below stay inside these ranges and needn't reach their ends.
All inputs are finite; a program needn't handle non-finite values.
Results may differ from the reference program's by a relative error of at most 0.017.
Values may be sent and summed in bfloat16 or wider, within the bound.
No kernel may reach another device: no remote copies, remote signals or barrier semaphores. Data moves between devices by JAX's collectives and lax.ppermute only.
A program may use at most 128 MiB of HBM per device.

```python
import jax
import jax.numpy as jnp
from jax import lax

D = 3072
HEADS = 12
HEAD = 128
TOK_DEV = 32
MB = 4
HD = 1536
LAYERS = 4
GROUPS = 16
ROWS = 2048


def place_ends(values, key, smallest, top_value):
    place = [jax.random.randint(jax.random.fold_in(key, axis), (), 0, length) for axis, length in enumerate(values.shape)]
    widest = values.shape.index(max(values.shape))
    next_to = place[:widest] + [(place[widest] + 1) % values.shape[widest]] + place[widest + 1:]
    return values.at[tuple(place)].set(smallest).at[tuple(next_to)].set(top_value)


def block_levels(key, extent, cuts, least, high):
    loudness = 1.0
    for dim, shards_of in cuts:
        heights = jax.random.uniform(jax.random.fold_in(jax.random.fold_in(key, 6), dim), (shards_of,), jnp.float32, least / len(cuts), high / len(cuts))
        loudness = loudness * jnp.repeat(jnp.exp(heights), extent[dim] // shards_of).reshape((-1,) + (1,) * (len(extent) - 1 - dim))
    return loudness


def noise(rng, dims, deviation, limit, cuts=(), kind=jnp.bfloat16):
    array = deviation * jax.random.normal(rng, dims, jnp.float32)
    if cuts:
        array = array * block_levels(rng, dims, cuts, -0.22, 0.18)
    return jnp.clip(array, -limit, limit).astype(kind)


def setup_inputs(seed: int = 0) -> dict:
    key_of = jax.random.split(jax.random.key(seed), 8)
    return {
        "hidden": noise(key_of[0], (MB, ROWS, D), 1.0, 6.0, ((1, 64),)),
        "w_query": noise(key_of[1], (LAYERS, 2, D, HD), D ** -0.5, 0.109375, ((0, 4), (2, 64))),
        "w_key": noise(key_of[2], (LAYERS, 2, D, HD), D ** -0.5, 0.109375, ((0, 4), (2, 64))),
        "w_value": noise(key_of[3], (LAYERS, 2, D, HD), D ** -0.5, 0.109375, ((0, 4), (2, 64))),
        "w_out": noise(key_of[4], (LAYERS, 2, HD, D), HD ** -0.5, 0.15625, ((0, 4), (3, 64))),
        "video_len": place_ends(jax.random.randint(key_of[5], (MB, GROUPS), 1, 3 * TOK_DEV + 1), jax.random.fold_in(key_of[5], 1), 1, 3 * TOK_DEV).astype(jnp.int32),
        "audio_len": place_ends(jax.random.randint(key_of[6], (MB, GROUPS), 1, TOK_DEV + 1), jax.random.fold_in(key_of[6], 1), 1, TOK_DEV).astype(jnp.int32),
    }


def rms_norm(values):
    wide = values.astype(jnp.float32)
    scale = lax.rsqrt(lax.optimization_barrier(jnp.mean(wide * wide, axis=-1, keepdims=True)) + 1e-06)
    return (wide * scale).astype(jnp.bfloat16)

def project(rows, weight, factor):
    return (jnp.dot(rows, weight, preferred_element_type=jnp.float32) * factor).astype(jnp.bfloat16)

def attend(query, keys, values, valid):
    groups, queries = (query.shape[0], query.shape[1])
    kcount = keys.shape[1]
    heads = query.reshape(groups, queries, HEADS, HEAD).astype(jnp.float32)
    keyed = keys.reshape(groups, kcount, HEADS, HEAD).astype(jnp.float32)
    valued = values.reshape(groups, kcount, HEADS, HEAD).astype(jnp.float32)
    scores = jnp.einsum('gqhd,gkhd->ghqk', heads, keyed)
    scores = jnp.where(valid[:, None, None, :], scores, -1e+30)
    weights = jax.nn.softmax(scores, axis=-1).astype(jnp.bfloat16).astype(jnp.float32)
    attended = jnp.einsum('ghqk,gkhd->gqhd', weights, valued).astype(jnp.bfloat16)
    return attended.reshape(groups * queries, HD)

def output(attended, weight):
    quarter = HD // 4
    pieces = attended.reshape(-1, 4, quarter).astype(jnp.float32)
    blocks = jnp.einsum('nck,ckd->cnd', pieces, weight.reshape(4, quarter, D).astype(jnp.float32))
    blocks = lax.optimization_barrier(blocks.astype(jnp.bfloat16))
    return lax.optimization_barrier(jnp.sum(blocks.astype(jnp.float32), axis=0))

def apply_block(state, w_query, w_key, w_value, w_out, video_count, audio_count):
    grouped = state.reshape(GROUPS, 4 * TOK_DEV, D)
    normed = rms_norm(grouped)
    video_rows = normed[:, :3 * TOK_DEV].reshape(-1, D)
    audio_rows = normed[:, 3 * TOK_DEV:].reshape(-1, D)
    factor = HEAD ** (-0.5)
    video_query = project(video_rows, w_query[0], factor).reshape(GROUPS, 3 * TOK_DEV, HD)
    audio_query = project(audio_rows, w_query[1], factor).reshape(GROUPS, TOK_DEV, HD)
    video_key = project(audio_rows, w_key[0], 1.0).reshape(GROUPS, TOK_DEV, HD)
    video_value = project(audio_rows, w_value[0], 1.0).reshape(GROUPS, TOK_DEV, HD)
    audio_key = project(video_rows, w_key[1], 1.0).reshape(GROUPS, 3 * TOK_DEV, HD)
    audio_value = project(video_rows, w_value[1], 1.0).reshape(GROUPS, 3 * TOK_DEV, HD)
    audio_valid = jnp.arange(TOK_DEV, dtype=jnp.int32)[None, :] < audio_count[:, None]
    video_valid = jnp.arange(3 * TOK_DEV, dtype=jnp.int32)[None, :] < video_count[:, None]
    video_att = attend(video_query, video_key, video_value, audio_valid)
    audio_att = attend(audio_query, audio_key, audio_value, video_valid)
    video_upd = output(video_att, w_out[0]).reshape(GROUPS, 3 * TOK_DEV, D)
    audio_upd = output(audio_att, w_out[1]).reshape(GROUPS, TOK_DEV, D)
    update = jnp.concatenate([video_upd, audio_upd], axis=1)
    return (grouped.astype(jnp.float32) + update).astype(jnp.bfloat16).reshape(ROWS, D)

def reference(hidden, w_query, w_key, w_value, w_out, video_len, audio_len):
    results = []
    for batch in range(MB):
        state = hidden[batch]
        for layer in range(LAYERS):
            state = apply_block(state, w_query[layer], w_key[layer], w_value[layer], w_out[layer], video_len[batch], audio_len[batch])
        results.append(state)
    return jnp.stack(results)
```

```python
import functools

import jax
import jax.numpy as jnp
from jax import lax
from jax.experimental import pallas as pl
from jax.experimental.pallas import tpu as pltpu
from jax.sharding import Mesh
from jax.sharding import PartitionSpec as P

HEAD = 128
NEAR = [(0, 1), (1, 0), (2, 3), (3, 2)]
FAR = [(1, 2), (2, 1), (3, 0), (0, 3)]
SWAP = [(0, 1), (1, 0)]


def rms_norm(values):
    wide = values.astype(jnp.float32)
    scale = lax.rsqrt(jnp.mean(wide * wide, axis=-1, keepdims=True) + 1e-06)
    return (wide * scale).astype(jnp.bfloat16)


def near(value):
    return lax.ppermute(value, "y", NEAR)


def far(value):
    return lax.ppermute(value, "y", FAR)


def swap(value):
    return lax.ppermute(value, "core", SWAP)


def attend_kernel(ctl, query, keys, values, out, *, tokens):
    rows = 4 * tokens
    flip, core = ctl[0], ctl[1]
    heads = query.shape[1] // HEAD
    key_place = lax.broadcasted_iota(jnp.int32, (rows, rows), 1) ^ flip
    query_place = lax.broadcasted_iota(jnp.int32, (rows, HEAD), 0) ^ flip
    video = 3 * tokens
    first = jnp.where(core == 0, video, 0)
    own_low = jnp.where(core == 0, 0, video)
    own_high = jnp.where(core == 0, video, rows)
    own = (query_place >= own_low) & (query_place < own_high)
    for sample in range(2):
        valid = (key_place >= first) & (key_place < first + ctl[2 + sample])
        span = pl.ds(sample * rows, rows)
        for head in range(heads):
            cols = pl.ds(head * HEAD, HEAD)
            scores = lax.dot_general(
                query[span, cols],
                keys[span, cols],
                (((1,), (1,)), ((), ())),
                preferred_element_type=jnp.float32,
            )
            scores = jnp.where(valid, scores, -1e30)
            top = jnp.max(scores, axis=-1, keepdims=True)
            powers = jnp.exp(scores - top)
            weights = (powers / jnp.sum(powers, axis=-1, keepdims=True)).astype(jnp.bfloat16)
            mixed = jnp.dot(weights, values[span, cols], preferred_element_type=jnp.float32)
            out[span, cols] = jnp.where(own, mixed, 0.0).astype(jnp.bfloat16)


def attend(ctl, query, keys, values, tokens):
    vmem = pl.BlockSpec(memory_space=pltpu.VMEM)
    return pl.pallas_call(
        functools.partial(attend_kernel, tokens=tokens),
        out_shape=jax.ShapeDtypeStruct(query.shape, jnp.bfloat16),
        in_specs=[pl.BlockSpec(memory_space=pltpu.SMEM), vmem, vmem, vmem],
        out_specs=vmem,
        cost_estimate=pl.CostEstimate(
            flops=4 * 128 * query.size, bytes_accessed=8 * query.size, transcendentals=query.size
        ),
    )(ctl, query, keys, values)


def gather_tokens(mine):
    half = mine.shape[0] // 2
    by_near, by_far = near(mine), far(mine)
    cross = jnp.concatenate([near(by_far[:half]), far(by_near[half:])])
    owned = jnp.stack([mine, by_near, cross, by_far])
    other = jnp.stack([swap(mine), swap(by_near), swap(cross), swap(by_far)])
    both = jnp.stack([owned, other], axis=1)
    return both.reshape(-1, mine.shape[1])


def reduce_tokens(state, partial_value):
    tokens, width = state.shape
    blocks = partial_value.reshape(4, 2, tokens, width)
    half = tokens // 2
    arrived = swap(blocks[:, 1])
    total = blocks[:, 0] + arrived
    low = near(total[2, :half]).astype(jnp.float32)
    high = far(total[2, half:]).astype(jnp.float32)
    to_far = jnp.concatenate(
        [(total[3, :half].astype(jnp.float32) + low).astype(jnp.bfloat16), total[3, half:]]
    )
    to_near = jnp.concatenate(
        [total[1, :half], (total[1, half:].astype(jnp.float32) + high).astype(jnp.bfloat16)]
    )
    by_near, by_far = near(to_near), far(to_far)
    update = total[0].astype(jnp.float32) + by_near.astype(jnp.float32) + by_far.astype(jnp.float32)
    return (state.astype(jnp.float32) + update).astype(jnp.bfloat16)


def body(hidden, w_query, w_key, w_value, w_out, video_len, audio_len):
    batch = lax.axis_index("pipe")
    depth = lax.axis_index("z")
    ring = lax.axis_index("y")
    core = lax.axis_index("core")
    batches, tokens, width = hidden.shape
    features = w_query.shape[3]
    rows = w_query.shape[2]
    quarter = features // 4
    layers = 4
    factor = HEAD ** (-0.5)
    turned = jnp.transpose(w_out[0], (0, 2, 1))
    parts = jnp.stack([w_query[0], w_key[0], w_value[0], turned])
    parts = parts.reshape(4, 2, rows, 4, quarter).transpose(0, 3, 1, 2, 4)
    parts = parts.reshape(32, rows, quarter)
    moved = lax.all_to_all(parts, ("pipe", "y", "core"), 0, 0, tiled=True)
    moved = moved.reshape(layers, 8 * rows, quarter)
    gathered = [
        lax.all_gather(moved[layer], ("pipe", "z"), axis=0).reshape(4, width, quarter)
        for layer in range(layers)
    ]
    state = lax.dynamic_index_in_dim(hidden, batch, 0, keepdims=False)
    low, high = ring % 2, ring // 2
    lengths = jnp.where(core == 0, audio_len[batch], video_len[batch])
    flip = 2 * tokens * low + tokens * core
    ctl = jnp.stack(
        [flip, core, lengths[2 * depth + high], lengths[2 * depth + 1 - high]]
    ).astype(jnp.int32)
    for layer in range(layers):
        weights = gathered[layer]
        normed = gather_tokens(rms_norm(state))

        def project(index, scale):
            made = jnp.dot(normed, weights[index], preferred_element_type=jnp.float32)
            return (made * scale).astype(jnp.bfloat16)

        attended = attend(ctl, project(0, factor), project(1, 1.0), project(2, 1.0), tokens)
        partial_value = lax.dot_general(
            attended, weights[3], (((1,), (1,)), ((), ())), preferred_element_type=jnp.float32
        ).astype(jnp.bfloat16)
        state = reduce_tokens(state, partial_value)
    return state[None]


def solution(mesh):
    inner = Mesh(mesh.devices.reshape(4, 8, 4, 2), ("pipe", "z", "y", "core"))
    dp = ("z", "y", "core")
    return jax.shard_map(
        body,
        mesh=inner,
        in_specs=(
            P(None, dp, None),
            P("pipe", None, dp, None),
            P("pipe", None, dp, None),
            P("pipe", None, dp, None),
            P("pipe", None, None, dp),
            P(),
            P(),
        ),
        out_specs=P("pipe", dp, None),
        check_vma=False,
    )
```

```python
import functools

import jax
import jax.numpy as jnp
from jax import lax
from jax.experimental import pallas as pl
from jax.experimental.pallas import tpu as pltpu
from jax.sharding import Mesh
from jax.sharding import PartitionSpec as P

HEAD = 128
NEAR = [(0, 1), (1, 0), (2, 3), (3, 2)]
FAR = [(1, 2), (2, 1), (3, 0), (0, 3)]
SWAP = [(0, 1), (1, 0)]


def rms_norm(values):
    wide = values.astype(jnp.float32)
    scale = lax.rsqrt(jnp.mean(wide * wide, axis=-1, keepdims=True) + 1e-06)
    return (wide * scale).astype(jnp.bfloat16)


def near(value):
    return lax.ppermute(value, "y", NEAR)


def far(value):
    return lax.ppermute(value, "y", FAR)


def swap(value):
    return lax.ppermute(value, "core", SWAP)


OFFSETS = (0, 7, 6, 5, 1, 2, 3, 4)


def block_kernel(ctl, *refs, tokens, along_depth, pieces):
    mine, by_near, by_far, cross, swapped, swapped_cross = refs[:6]
    weights = refs[6 : 6 + pieces]
    keep, give, held, normed, sums, mixed_all, sems = refs[6 + pieces :]
    size = held.shape[2]
    copies = []
    if along_depth:
        for slot in range(7):
            copies.append([pltpu.make_async_copy(weights[slot], held.at[slot], sems.at[slot])])
        copies.append(
            [
                pltpu.make_async_copy(weights[7], held.at[7, 0:2], sems.at[7]),
                pltpu.make_async_copy(weights[8], held.at[7, 2:4], sems.at[8]),
            ]
        )
    else:
        for slot, source in ((0, 0), (1, 1), (3, 2)):
            copies.append([pltpu.make_async_copy(weights[source], held.at[slot], sems.at[slot])])
        copies.insert(
            2,
            [
                pltpu.make_async_copy(weights[3], held.at[2, 0:4], sems.at[2]),
                pltpu.make_async_copy(weights[4], held.at[2, 4:8], sems.at[4]),
            ],
        )
    for group in copies:
        for copy in group:
            copy.start()
    flip, core, section, depth = ctl[0], ctl[1], ctl[4], ctl[5]
    for block, (own, other) in enumerate(
        ((mine, swapped.at[0]), (by_near, swapped.at[1]), (cross, swapped_cross), (by_far, swapped.at[2]))
    ):
        normed[pl.ds(2 * block * tokens, tokens), :] = own[...]
        normed[pl.ds((2 * block + 1) * tokens, tokens), :] = other[...]
    sums[...] = jnp.zeros_like(sums)

    def columns(slot):
        place = (depth + ctl[8 + slot]) & 7
        return pl.ds(pl.multiple_of(place * size, 128), size)

    def add(outer, inner):
        index, slot = (inner, outer) if along_depth else (outer, inner)
        array = section ^ index

        @pl.when(array != 3)
        def _():
            sums[array] += jnp.dot(
                normed[:, columns(slot)], held[outer, inner], preferred_element_type=jnp.float32
            )

    for outer, group in enumerate(copies):
        for copy in group:
            copy.wait()
        pl.loop(0, held.shape[1])(functools.partial(add, outer))

    rows = 4 * tokens
    heads = size // HEAD
    key_place = lax.broadcasted_iota(jnp.int32, (rows, rows), 1) ^ flip
    query_place = lax.broadcasted_iota(jnp.int32, (rows, HEAD), 0) ^ flip
    video = 3 * tokens
    first = jnp.where(core == 0, video, 0)
    own_low = jnp.where(core == 0, 0, video)
    own_high = jnp.where(core == 0, video, rows)
    live = (query_place >= own_low) & (query_place < own_high)
    for sample in range(2):
        valid = (key_place >= first) & (key_place < first + ctl[2 + sample])
        span = pl.ds(sample * rows, rows)
        for head in range(heads):
            cols = pl.ds(head * HEAD, HEAD)
            scores = lax.dot_general(
                (sums[0, span, cols] * HEAD ** (-0.5)).astype(jnp.bfloat16),
                sums[1, span, cols].astype(jnp.bfloat16),
                (((1,), (1,)), ((), ())),
                preferred_element_type=jnp.float32,
            )
            scores = jnp.where(valid, scores, -1e30)
            top = jnp.max(scores, axis=-1, keepdims=True)
            powers = jnp.exp(scores - top)
            shares = (powers / jnp.sum(powers, axis=-1, keepdims=True)).astype(jnp.bfloat16)
            mixed = jnp.dot(
                shares, sums[2, span, cols].astype(jnp.bfloat16), preferred_element_type=jnp.float32
            )
            mixed_all[span, cols] = jnp.where(live, mixed, 0.0).astype(jnp.bfloat16)
    last = section ^ 3

    @pl.loop(0, 8)
    def _(slot):
        piece = held[slot, last] if along_depth else held[last, slot]
        made = lax.dot_general(
            mixed_all[...], piece, (((1,), (1,)), ((), ())), preferred_element_type=jnp.float32
        ).astype(jnp.bfloat16)
        for block in range(4):
            keep[block, :, columns(slot)] = made[2 * block * tokens : (2 * block + 1) * tokens]
            give[block, :, columns(slot)] = made[(2 * block + 1) * tokens : (2 * block + 2) * tokens]


def run_block(ctl, blocks, weights, tokens, width, along_depth):
    size = weights[0].shape[1]
    vmem = pl.BlockSpec(memory_space=pltpu.VMEM)
    there = pl.BlockSpec(memory_space=pl.ANY)
    shape = (8, 4, size, size) if along_depth else (4, 8, size, size)
    out = jax.ShapeDtypeStruct((4, tokens, width), jnp.bfloat16)
    count = 8 * tokens
    return pl.pallas_call(
        functools.partial(
            block_kernel, tokens=tokens, along_depth=along_depth, pieces=len(weights)
        ),
        out_shape=(out, out),
        in_specs=[pl.BlockSpec(memory_space=pltpu.SMEM)] + [vmem] * 6 + [there] * len(weights),
        out_specs=(vmem, vmem),
        scratch_shapes=[
            pltpu.VMEM(shape, jnp.bfloat16),
            pltpu.VMEM((count, width), jnp.bfloat16),
            pltpu.VMEM((3, count, size), jnp.float32),
            pltpu.VMEM((count, size), jnp.bfloat16),
            pltpu.SemaphoreType.DMA((9,)),
        ],
        compiler_params=pltpu.CompilerParams(vmem_limit_bytes=24 << 20),
        cost_estimate=pl.CostEstimate(
            flops=8 * count * width * size,
            bytes_accessed=8 * width * size + 6 * count * width,
            transcendentals=count * size,
        ),
    )(ctl, *blocks, *weights)


def gather_tokens(mine):
    by_near, by_far = near(mine), far(mine)
    cross = near(by_far)
    return mine, by_near, by_far, cross, swap(jnp.stack([mine, by_near, by_far])), swap(cross)


def reduce_tokens(state, keep, give):
    total = keep + swap(give)
    passed = near(total[2])
    by_near = near(total[1])
    to_far = (total[3].astype(jnp.float32) + passed.astype(jnp.float32)).astype(jnp.bfloat16)
    by_far = far(to_far)
    update = total[0].astype(jnp.float32) + by_near.astype(jnp.float32) + by_far.astype(jnp.float32)
    return (state.astype(jnp.float32) + update).astype(jnp.bfloat16)


def up(value):
    return lax.ppermute(value, "z", [(place, (place + 1) % 8) for place in range(8)])


def down(value):
    return lax.ppermute(value, "z", [(place, (place - 1) % 8) for place in range(8)])


def beside(value):
    return lax.ppermute(value, "pipe", NEAR)


def around(value):
    return lax.ppermute(value, "pipe", FAR)


def spread_across_then_deep(shard):
    by_beside, by_around = beside(shard), around(shard)
    four = jnp.stack([shard, by_beside, beside(by_around), by_around])
    below = [up(four)]
    above = [down(four)]
    for _ in range(2):
        below.append(up(below[-1]))
        above.append(down(above[-1]))
    return [four, *below, *above, up(below[-1][:2]), down(above[-1][2:])]


def spread_deep_then_across(shard):
    below = [up(shard)]
    above = [down(shard)]
    for _ in range(2):
        below.append(up(below[-1]))
        above.append(down(above[-1]))
    eight = jnp.stack([shard, *below, *above, down(above[-1])])
    by_beside, by_around = beside(eight), around(eight)
    return [eight, by_beside, by_around, beside(by_around[:4]), around(by_beside[4:])]


def body(hidden, w_query, w_key, w_value, w_out, video_len, audio_len):
    batch = lax.axis_index("pipe")
    depth = lax.axis_index("z")
    ring = lax.axis_index("y")
    core = lax.axis_index("core")
    batches, tokens, width = hidden.shape
    features = w_query.shape[3]
    rows = w_query.shape[2]
    quarter = features // 4
    layers = 4
    turned = jnp.transpose(w_out[0], (0, 2, 1))
    parts = jnp.stack([w_query[0], w_key[0], w_value[0], turned])
    parts = parts.reshape(4, 2, rows, 4, quarter).transpose(0, 3, 1, 2, 4)
    parts = parts.reshape(32, rows, quarter)
    moved = lax.all_to_all(parts, ("pipe", "y", "core"), 0, 0, tiled=True)
    moved = moved.reshape(layers, 8 * rows, quarter)
    gathered = [
        (spread_deep_then_across if layer % 2 else spread_across_then_deep)(moved[layer])
        for layer in range(layers)
    ]
    state = lax.dynamic_index_in_dim(hidden, batch, 0, keepdims=False)
    low, high = ring % 2, ring // 2
    lengths = jnp.where(core == 0, audio_len[batch], video_len[batch])
    flip = 2 * tokens * low + tokens * core
    zero = jnp.int32(0)
    ctl = jnp.stack(
        [flip, core, lengths[2 * depth + high], lengths[2 * depth + 1 - high], batch, depth, zero, zero]
        + [jnp.int32(step) for step in OFFSETS]
    ).astype(jnp.int32)
    for layer in range(layers):
        blocks = gather_tokens(rms_norm(state))
        keep, give = run_block(ctl, blocks, gathered[layer], tokens, width, layer % 2 == 0)
        state = reduce_tokens(state, keep, give)
    return state[None]


def solution(mesh):
    inner = Mesh(mesh.devices.reshape(4, 8, 4, 2), ("pipe", "z", "y", "core"))
    dp = ("z", "y", "core")
    return jax.shard_map(
        body,
        mesh=inner,
        in_specs=(
            P(None, dp, None),
            P("pipe", None, dp, None),
            P("pipe", None, dp, None),
            P("pipe", None, dp, None),
            P("pipe", None, None, dp),
            P(),
            P(),
        ),
        out_specs=P("pipe", dp, None),
        check_vma=False,
    )
```

```python
import functools

import jax
import jax.numpy as jnp
from jax import lax
from jax.experimental import pallas as pl
from jax.experimental.pallas import tpu as pltpu
from jax.sharding import Mesh
from jax.sharding import PartitionSpec as P

HEAD = 128
NEAR = [(0, 1), (1, 0), (2, 3), (3, 2)]
FAR = [(1, 2), (2, 1), (3, 0), (0, 3)]
SWAP = [(0, 1), (1, 0)]


def rms_norm(values):
    wide = values.astype(jnp.float32)
    scale = lax.rsqrt(jnp.mean(wide * wide, axis=-1, keepdims=True) + 1e-06)
    return (wide * scale).astype(jnp.bfloat16)


def near(value):
    return lax.ppermute(value, "y", NEAR)


def far(value):
    return lax.ppermute(value, "y", FAR)


def swap(value):
    return lax.ppermute(value, "core", SWAP)


def up(value):
    return lax.ppermute(value, "z", [(place, (place + 1) % 8) for place in range(8)])


def down(value):
    return lax.ppermute(value, "z", [(place, (place - 1) % 8) for place in range(8)])


def beside(value):
    return lax.ppermute(value, "pipe", NEAR)


def around(value):
    return lax.ppermute(value, "pipe", FAR)


SHALLOW = (256, 0, 128, 256)
OFFSETS = (0, 7, 6, 5, 1, 2, 3, 4)


def block_kernel(ctl, *refs, tokens, shallow, pieces):
    mine, by_near, by_far, cross, swapped, swapped_cross = refs[:6]
    weights = refs[6 : 6 + pieces]
    keep, give, held, normed, sums, mixed_all, sems = refs[6 + pieces :]
    size = sums.shape[2]
    places = []
    if shallow:
        rows = pl.ds(0, shallow)
        places += [held.at[:, slot, rows] for slot in range(7)]
        places += [held.at[0:2, 7, rows], held.at[2:4, 7, rows]]
    if shallow < size:
        rows = pl.ds(shallow, size - shallow)
        places += [held.at[index // 2, pl.ds(index % 2 * 4, 4), rows] for index in range(8)]
    copies = [
        pltpu.make_async_copy(weights[index], place, sems.at[index])
        for index, place in enumerate(places)
    ]
    for copy in copies:
        copy.start()
    flip, core, section, depth = ctl[0], ctl[1], ctl[4], ctl[5]

    def columns(slot):
        place = (depth + ctl[8 + slot]) & 7
        return pl.ds(pl.multiple_of(place * size, 128), size)

    for slot in range(8):
        cols, to = columns(slot), pl.ds(slot * size, size)
        for block, (own, other) in enumerate(
            ((mine, swapped.at[0]), (by_near, swapped.at[1]), (cross, swapped_cross), (by_far, swapped.at[2]))
        ):
            normed[pl.ds(2 * block * tokens, tokens), to] = own[:, cols]
            normed[pl.ds((2 * block + 1) * tokens, tokens), to] = other[:, cols]

    for copy in copies:
        copy.wait()
    for index in range(4):
        array = section ^ index

        @pl.when(array != 3)
        def _():
            sums[array] = jnp.dot(
                normed[...],
                held[index].reshape(8 * size, size),
                preferred_element_type=jnp.float32,
            )

    rows = 4 * tokens
    heads = size // HEAD
    key_place = lax.broadcasted_iota(jnp.int32, (rows, rows), 1) ^ flip
    query_place = lax.broadcasted_iota(jnp.int32, (rows, HEAD), 0) ^ flip
    video = 3 * tokens
    first = jnp.where(core == 0, video, 0)
    own_low = jnp.where(core == 0, 0, video)
    own_high = jnp.where(core == 0, video, rows)
    live = (query_place >= own_low) & (query_place < own_high)
    for sample in range(2):
        valid = (key_place >= first) & (key_place < first + ctl[2 + sample])
        span = pl.ds(sample * rows, rows)
        spans = [pl.ds(head * HEAD, HEAD) for head in range(heads)]
        scores = [
            lax.dot_general(
                (sums[0, span, cols] * HEAD ** (-0.5)).astype(jnp.bfloat16),
                sums[1, span, cols].astype(jnp.bfloat16),
                (((1,), (1,)), ((), ())),
                preferred_element_type=jnp.float32,
            )
            for cols in spans
        ]
        scores = [jnp.where(valid, score, -1e30) for score in scores]
        powers = [jnp.exp(score - jnp.max(score, axis=-1, keepdims=True)) for score in scores]
        shares = [
            (power * (1.0 / jnp.sum(power, axis=-1, keepdims=True))).astype(jnp.bfloat16)
            for power in powers
        ]
        mixed = [
            jnp.dot(share, sums[2, span, cols].astype(jnp.bfloat16), preferred_element_type=jnp.float32)
            for share, cols in zip(shares, spans)
        ]
        for head, cols in enumerate(spans):
            mixed_all[span, cols] = jnp.where(live, mixed[head], 0.0).astype(jnp.bfloat16)
    last = section ^ 3

    def project(piece, slot):
        made = lax.dot_general(
            mixed_all[...], piece, (((1,), (1,)), ((), ())), preferred_element_type=jnp.float32
        ).astype(jnp.bfloat16)
        for block in range(4):
            keep[block, :, columns(slot)] = made[2 * block * tokens : (2 * block + 1) * tokens]
            give[block, :, columns(slot)] = made[(2 * block + 1) * tokens : (2 * block + 2) * tokens]

    @pl.loop(0, 8)
    def _(slot):
        project(held[last, slot], slot)


def run_block(ctl, blocks, weights, tokens, width, shallow):
    size = weights[0].shape[2]
    vmem = pl.BlockSpec(memory_space=pltpu.VMEM)
    out = jax.ShapeDtypeStruct((4, tokens, width), jnp.bfloat16)
    count = 8 * tokens
    there = pl.BlockSpec(memory_space=pltpu.HBM)
    return pl.pallas_call(
        functools.partial(
            block_kernel, tokens=tokens, shallow=shallow, pieces=len(weights)
        ),
        out_shape=(out, out),
        in_specs=[pl.BlockSpec(memory_space=pltpu.SMEM)] + [vmem] * 6 + [there] * len(weights),
        out_specs=(vmem, vmem),
        scratch_shapes=[
            pltpu.VMEM((4, 8, size, size), jnp.bfloat16),
            pltpu.VMEM((count, width), jnp.bfloat16),
            pltpu.VMEM((3, count, size), jnp.float32),
            pltpu.VMEM((count, size), jnp.bfloat16),
            pltpu.SemaphoreType.DMA((17,)),
        ],
        compiler_params=pltpu.CompilerParams(vmem_limit_bytes=24 << 20),
        cost_estimate=pl.CostEstimate(
            flops=8 * count * width * size,
            bytes_accessed=8 * width * size + 6 * count * width,
            transcendentals=count * size,
        ),
    )(ctl, *blocks, *weights)


def pack_kernel(query, key, value, out, packed):
    quarter = packed.shape[4]
    for tower in range(2):
        for part in range(4):
            cols = pl.ds(part * quarter, quarter)
            packed[0, part, tower] = query[tower, :, cols]
            packed[1, part, tower] = key[tower, :, cols]
            packed[2, part, tower] = value[tower, :, cols]
            packed[3, part, tower] = out[tower, cols, :].T


def pack(query, key, value, out):
    towers, rows, features = query.shape
    vmem = pl.BlockSpec(memory_space=pltpu.VMEM)
    return pl.pallas_call(
        pack_kernel,
        out_shape=jax.ShapeDtypeStruct((4, 4, towers, rows, features // 4), jnp.bfloat16),
        in_specs=[vmem] * 4,
        out_specs=vmem,
    )(query, key, value, out)


def gather_tokens(mine):
    half = mine.shape[0] // 2
    by_near, by_far = near(mine), far(mine)
    pair = swap(jnp.stack([mine, by_near, by_far]))
    cross = jnp.concatenate([near(by_far[:half]), far(by_near[half:])])
    return mine, by_near, by_far, cross, pair, swap(cross)


def reduce_tokens(state, keep, give):
    half = state.shape[0] // 2
    total = keep + swap(give)
    low = near(total[2, :half]).astype(jnp.float32)
    high = far(total[2, half:]).astype(jnp.float32)
    to_far = jnp.concatenate(
        [(total[3, :half].astype(jnp.float32) + low).astype(jnp.bfloat16), total[3, half:]]
    )
    to_near = jnp.concatenate(
        [total[1, :half], (total[1, half:].astype(jnp.float32) + high).astype(jnp.bfloat16)]
    )
    by_near, by_far = near(to_near), far(to_far)
    update = total[0].astype(jnp.float32) + by_near.astype(jnp.float32) + by_far.astype(jnp.float32)
    return (state.astype(jnp.float32) + update).astype(jnp.bfloat16)


def across(shard):
    by_beside, by_around = beside(shard), around(shard)
    return jnp.stack([shard, by_beside, beside(by_around), by_around])


def deep(block):
    below = [up(block)]
    above = [down(block)]
    for _ in range(2):
        below.append(up(below[-1]))
        above.append(down(above[-1]))
    return below, above


def finish_deep(four):
    below, above = deep(four)
    return [four, *below, *above, up(below[-1][:2]), down(above[-1][2:])]


def finish_across(lower, upper):
    by_beside = beside(lower), beside(upper)
    by_around = around(lower), around(upper)
    crossed = beside(by_around[0]), around(by_beside[1])
    return [lower, upper, *by_beside, *crossed, *by_around]


def spread(shards):
    zero, one, two, three = shards
    cut = SHALLOW
    size = zero.shape[0]
    shallow = [finish_deep(across(zero[: cut[0]])), []]
    both = across(jnp.concatenate([two[: cut[2]], three[: cut[3]]]))
    shallow.append(finish_deep(both[:, : cut[2]]))
    shallow.append(finish_deep(both[:, cut[2] :]))
    rest = zero[cut[0] :]
    below, above = deep(rest)
    lower = jnp.stack([rest, *below])
    upper = jnp.stack([*above, up(below[-1])])
    across_all = [finish_across(lower, upper)]
    rest = jnp.concatenate([one, two[cut[2] :], three[cut[3] :]])
    below, above = deep(rest)
    ends = up(below[-1][:size]), down(above[-1][size:])
    start = 0
    for layer in (1, 2, 3):
        stop = start + size - cut[layer]
        end = ends[0] if layer == 1 else ends[1][start - size : stop - size]
        lower = jnp.stack([part[start:stop] for part in [rest, *below]])
        upper = jnp.stack([part[start:stop] for part in above] + [end])
        across_all.append(finish_across(lower, upper))
        start = stop
    return [early + late for early, late in zip(shallow, across_all)]


def section(hidden, w_query, w_key, w_value, w_out, video_len, audio_len):
    batch = lax.axis_index("pipe")
    depth = lax.axis_index("z")
    ring = lax.axis_index("y")
    core = lax.axis_index("core")
    _, tokens, width = hidden.shape
    features = w_query.shape[3]
    rows = w_query.shape[2]
    quarter = features // 4
    layers = 4
    parts = pack(w_query[0], w_key[0], w_value[0], w_out[0]).reshape(32, rows, quarter)
    moved = lax.all_to_all(parts, ("pipe", "y", "core"), 0, 0, tiled=True)
    moved = moved.reshape(layers, 8 * rows, quarter)
    gathered = spread(moved)
    state = lax.dynamic_index_in_dim(hidden, batch, 0, keepdims=False)
    low, high = ring % 2, ring // 2
    lengths = jnp.where(core == 0, audio_len[batch], video_len[batch])
    flip = 2 * tokens * low + tokens * core
    zero = jnp.int32(0)
    ctl = jnp.stack(
        [flip, core, lengths[2 * depth + high], lengths[2 * depth + 1 - high], batch, depth, zero, zero]
        + [jnp.int32(offset) for offset in OFFSETS]
    ).astype(jnp.int32)
    for layer in range(layers):
        blocks = gather_tokens(rms_norm(state))
        keep, give = run_block(ctl, blocks, gathered[layer], tokens, width, SHALLOW[layer])
        state = reduce_tokens(state, keep, give)
    return state[None]


def solution(mesh):
    inner = Mesh(mesh.devices.reshape(4, 8, 4, 2), ("pipe", "z", "y", "core"))
    dp = ("z", "y", "core")
    return jax.shard_map(
        section,
        mesh=inner,
        in_specs=(
            P(None, dp, None),
            P("pipe", None, dp, None),
            P("pipe", None, dp, None),
            P("pipe", None, dp, None),
            P("pipe", None, None, dp),
            P(),
            P(),
        ),
        out_specs=P("pipe", dp, None),
        check_vma=False,
    )
```

```python
import functools

import jax
import jax.numpy as jnp
from jax import lax
from jax.experimental import pallas as pl
from jax.experimental.pallas import tpu as pltpu
from jax.sharding import Mesh
from jax.sharding import PartitionSpec as P

HEAD = 128
NEAR = [(0, 1), (1, 0), (2, 3), (3, 2)]
FAR = [(1, 2), (2, 1), (3, 0), (0, 3)]
SWAP = [(0, 1), (1, 0)]


def rms_norm(values):
    wide = values.astype(jnp.float32)
    scale = lax.rsqrt(jnp.mean(wide * wide, axis=-1, keepdims=True) + 1e-06)
    return (wide * scale).astype(jnp.bfloat16)


def near(value):
    return lax.ppermute(value, "y", NEAR)


def far(value):
    return lax.ppermute(value, "y", FAR)


def swap(value):
    return lax.ppermute(value, "core", SWAP)


def up(value):
    return lax.ppermute(value, "z", [(place, (place + 1) % 8) for place in range(8)])


def down(value):
    return lax.ppermute(value, "z", [(place, (place - 1) % 8) for place in range(8)])


def beside(value):
    return lax.ppermute(value, "pipe", NEAR)


def around(value):
    return lax.ppermute(value, "pipe", FAR)


SHALLOW = (256, 0, 128, 256)
OFFSETS = (0, 7, 6, 5, 1, 2, 3, 4)


def block_kernel(ctl, *refs, tokens, shallow, pieces):
    mine, by_near, by_far, cross, swapped, swapped_cross = refs[:6]
    weights = refs[6 : 6 + pieces]
    keep, give, held, normed, sums, mixed_all, sems = refs[6 + pieces :]
    size = sums.shape[2]
    places = []
    if shallow:
        rows = pl.ds(0, shallow)
        places += [held.at[:, slot, rows] for slot in range(7)]
        places += [held.at[0:2, 7, rows], held.at[2:4, 7, rows]]
    if shallow < size:
        rows = pl.ds(shallow, size - shallow)
        places += [held.at[index // 2, pl.ds(index % 2 * 4, 4), rows] for index in range(8)]
    copies = [
        pltpu.make_async_copy(weights[index], place, sems.at[index])
        for index, place in enumerate(places)
    ]
    for copy in copies:
        copy.start()
    flip, core, section, depth = ctl[0], ctl[1], ctl[4], ctl[5]

    def columns(slot):
        place = (depth + ctl[8 + slot]) & 7
        return pl.ds(pl.multiple_of(place * size, 128), size)

    @pl.loop(0, 8)
    def _(slot):
        cols, to = columns(slot), pl.ds(pl.multiple_of(slot * size, 128), size)
        for block, (own, other) in enumerate(
            ((mine, swapped.at[0]), (by_near, swapped.at[1]), (cross, swapped_cross), (by_far, swapped.at[2]))
        ):
            normed[pl.ds(2 * block * tokens, tokens), to] = own[:, cols]
            normed[pl.ds((2 * block + 1) * tokens, tokens), to] = other[:, cols]

    for copy in copies:
        copy.wait()

    @pl.loop(0, 4)
    def _(index):
        array = section ^ index

        @pl.when(array != 3)
        def _():
            sums[array] = jnp.dot(
                normed[...],
                held[index].reshape(8 * size, size),
                preferred_element_type=jnp.float32,
            )

    rows = 4 * tokens
    heads = size // HEAD
    key_place = lax.broadcasted_iota(jnp.int32, (rows, rows), 1) ^ flip
    query_place = lax.broadcasted_iota(jnp.int32, (rows, HEAD), 0) ^ flip
    video = 3 * tokens
    first = jnp.where(core == 0, video, 0)
    own_low = jnp.where(core == 0, 0, video)
    own_high = jnp.where(core == 0, video, rows)
    live = (query_place >= own_low) & (query_place < own_high)
    for sample in range(2):
        valid = (key_place >= first) & (key_place < first + ctl[2 + sample])
        span = pl.ds(sample * rows, rows)
        spans = [pl.ds(head * HEAD, HEAD) for head in range(heads)]
        scores = [
            lax.dot_general(
                (sums[0, span, cols] * HEAD ** (-0.5)).astype(jnp.bfloat16),
                sums[1, span, cols].astype(jnp.bfloat16),
                (((1,), (1,)), ((), ())),
                preferred_element_type=jnp.float32,
            )
            for cols in spans
        ]
        scores = [jnp.where(valid, score, -1e30) for score in scores]
        powers = [jnp.exp(score - jnp.max(score, axis=-1, keepdims=True)) for score in scores]
        shares = [
            (power * (1.0 / jnp.sum(power, axis=-1, keepdims=True))).astype(jnp.bfloat16)
            for power in powers
        ]
        mixed = [
            jnp.dot(share, sums[2, span, cols].astype(jnp.bfloat16), preferred_element_type=jnp.float32)
            for share, cols in zip(shares, spans)
        ]
        for head, cols in enumerate(spans):
            mixed_all[span, cols] = jnp.where(live, mixed[head], 0.0).astype(jnp.bfloat16)
    last = section ^ 3

    def project(piece, slot):
        made = lax.dot_general(
            mixed_all[...], piece, (((1,), (1,)), ((), ())), preferred_element_type=jnp.float32
        ).astype(jnp.bfloat16)
        for block in range(4):
            keep[block, :, columns(slot)] = made[2 * block * tokens : (2 * block + 1) * tokens]
            give[block, :, columns(slot)] = made[(2 * block + 1) * tokens : (2 * block + 2) * tokens]

    @pl.loop(0, 8)
    def _(slot):
        project(held[last, slot], slot)


def run_block(ctl, blocks, weights, tokens, width, shallow):
    size = weights[0].shape[2]
    vmem = pl.BlockSpec(memory_space=pltpu.VMEM)
    out = jax.ShapeDtypeStruct((4, tokens, width), jnp.bfloat16)
    count = 8 * tokens
    there = pl.BlockSpec(memory_space=pltpu.HBM)
    return pl.pallas_call(
        functools.partial(
            block_kernel, tokens=tokens, shallow=shallow, pieces=len(weights)
        ),
        out_shape=(out, out),
        in_specs=[pl.BlockSpec(memory_space=pltpu.SMEM)] + [vmem] * 6 + [there] * len(weights),
        out_specs=(vmem, vmem),
        scratch_shapes=[
            pltpu.VMEM((4, 8, size, size), jnp.bfloat16),
            pltpu.VMEM((count, width), jnp.bfloat16),
            pltpu.VMEM((3, count, size), jnp.float32),
            pltpu.VMEM((count, size), jnp.bfloat16),
            pltpu.SemaphoreType.DMA((17,)),
        ],
        compiler_params=pltpu.CompilerParams(vmem_limit_bytes=24 << 20),
        cost_estimate=pl.CostEstimate(
            flops=8 * count * width * size,
            bytes_accessed=8 * width * size + 6 * count * width,
            transcendentals=count * size,
        ),
    )(ctl, *blocks, *weights)


def pack_kernel(query, key, value, out, packed):
    quarter = packed.shape[4]
    for tower in range(2):
        for part in range(4):
            cols = pl.ds(part * quarter, quarter)
            packed[0, part, tower] = query[tower, :, cols]
            packed[1, part, tower] = key[tower, :, cols]
            packed[2, part, tower] = value[tower, :, cols]
            packed[3, part, tower] = out[tower, cols, :].T


def pack(query, key, value, out):
    towers, rows, features = query.shape
    vmem = pl.BlockSpec(memory_space=pltpu.VMEM)
    return pl.pallas_call(
        pack_kernel,
        out_shape=jax.ShapeDtypeStruct((4, 4, towers, rows, features // 4), jnp.bfloat16),
        in_specs=[vmem] * 4,
        out_specs=vmem,
    )(query, key, value, out)


def gather_tokens(mine):
    half = mine.shape[0] // 2
    by_near, by_far = near(mine), far(mine)
    pair = swap(jnp.stack([mine, by_near, by_far]))
    cross = jnp.concatenate([near(by_far[:half]), far(by_near[half:])])
    return mine, by_near, by_far, cross, pair, swap(cross)


def reduce_tokens(state, keep, give):
    half = state.shape[0] // 2
    total = keep + swap(give)
    low = near(total[2, :half]).astype(jnp.float32)
    high = far(total[2, half:]).astype(jnp.float32)
    to_far = jnp.concatenate(
        [(total[3, :half].astype(jnp.float32) + low).astype(jnp.bfloat16), total[3, half:]]
    )
    to_near = jnp.concatenate(
        [total[1, :half], (total[1, half:].astype(jnp.float32) + high).astype(jnp.bfloat16)]
    )
    by_near, by_far = near(to_near), far(to_far)
    update = total[0].astype(jnp.float32) + by_near.astype(jnp.float32) + by_far.astype(jnp.float32)
    return (state.astype(jnp.float32) + update).astype(jnp.bfloat16)


def across(shard):
    by_beside, by_around = beside(shard), around(shard)
    return jnp.stack([shard, by_beside, beside(by_around), by_around])


def deep(block):
    below = [up(block)]
    above = [down(block)]
    for _ in range(2):
        below.append(up(below[-1]))
        above.append(down(above[-1]))
    return below, above


def finish_deep(four):
    below, above = deep(four)
    return [four, *below, *above, up(below[-1][:2]), down(above[-1][2:])]


def finish_across(lower, upper, later):
    by_beside = beside(lower), beside(upper)
    by_around = around(lower), around(upper)
    passed, later = lax.optimization_barrier((by_around[0], later))
    crossed = beside(passed), around(by_beside[1])
    return [lower, upper, *by_beside, *crossed, by_around[0], by_around[1]], later


def spread(shards):
    zero, one, two, three = shards
    cut = SHALLOW
    size = zero.shape[0]
    shallow = [finish_deep(across(zero[: cut[0]])), []]
    both = across(jnp.concatenate([two[: cut[2]], three[: cut[3]]]))
    shallow.append(finish_deep(both[:, : cut[2]]))
    shallow.append(finish_deep(both[:, cut[2] :]))
    rest = zero[cut[0] :]
    below, above = deep(rest)
    lower = jnp.stack([rest, *below])
    upper = jnp.stack([*above, up(below[-1])])
    across_all = [finish_across(lower, upper, ())[0]]
    rest = jnp.concatenate([one, two[cut[2] :], three[cut[3] :]])
    below, above = deep(rest)
    ends = up(below[-1][:size]), down(above[-1][size:])
    start = 0
    stacks = []
    for layer in (1, 2, 3):
        stop = start + size - cut[layer]
        end = ends[0] if layer == 1 else ends[1][start - size : stop - size]
        stacks.append(
            (
                jnp.stack([part[start:stop] for part in [rest, *below]]),
                jnp.stack([part[start:stop] for part in above] + [end]),
            )
        )
        start = stop
    lower, upper = stacks[0]
    made, later = finish_across(lower, upper, stacks[1:])
    across_all.append(made)
    for layer, (lower, upper) in zip((2, 3), later):
        across_all.append(finish_across(lower, upper, ())[0])
    return [early + late for early, late in zip(shallow, across_all)]


def section(hidden, w_query, w_key, w_value, w_out, video_len, audio_len):
    batch = lax.axis_index("pipe")
    depth = lax.axis_index("z")
    ring = lax.axis_index("y")
    core = lax.axis_index("core")
    _, tokens, width = hidden.shape
    features = w_query.shape[3]
    rows = w_query.shape[2]
    quarter = features // 4
    layers = 4
    parts = pack(w_query[0], w_key[0], w_value[0], w_out[0]).reshape(32, rows, quarter)
    moved = lax.all_to_all(parts, ("pipe", "y", "core"), 0, 0, tiled=True)
    moved = moved.reshape(layers, 8 * rows, quarter)
    gathered = spread(moved)
    state = lax.dynamic_index_in_dim(hidden, batch, 0, keepdims=False)
    low, high = ring % 2, ring // 2
    lengths = jnp.where(core == 0, audio_len[batch], video_len[batch])
    flip = 2 * tokens * low + tokens * core
    zero = jnp.int32(0)
    ctl = jnp.stack(
        [flip, core, lengths[2 * depth + high], lengths[2 * depth + 1 - high], batch, depth, zero, zero]
        + [jnp.int32(offset) for offset in OFFSETS]
    ).astype(jnp.int32)
    for layer in range(layers):
        blocks = gather_tokens(rms_norm(state))
        keep, give = run_block(ctl, blocks, gathered[layer], tokens, width, SHALLOW[layer])
        state = reduce_tokens(state, keep, give)
    return state[None]


def solution(mesh):
    inner = Mesh(mesh.devices.reshape(4, 8, 4, 2), ("pipe", "z", "y", "core"))
    dp = ("z", "y", "core")
    return jax.shard_map(
        section,
        mesh=inner,
        in_specs=(
            P(None, dp, None),
            P("pipe", None, dp, None),
            P("pipe", None, dp, None),
            P("pipe", None, dp, None),
            P("pipe", None, None, dp),
            P(),
            P(),
        ),
        out_specs=P("pipe", dp, None),
        check_vma=False,
    )
```

```python
import functools

import jax
import jax.numpy as jnp
from jax import lax
from jax.experimental import pallas as pl
from jax.experimental.pallas import tpu as pltpu
from jax.sharding import Mesh
from jax.sharding import PartitionSpec as P

HEAD = 128
NEAR = [(0, 1), (1, 0), (2, 3), (3, 2)]
FAR = [(1, 2), (2, 1), (3, 0), (0, 3)]
SWAP = [(0, 1), (1, 0)]


def rms_norm(values):
    wide = values.astype(jnp.float32)
    scale = lax.rsqrt(jnp.mean(wide * wide, axis=-1, keepdims=True) + 1e-06)
    return (wide * scale).astype(jnp.bfloat16)


def near(value):
    return lax.ppermute(value, "y", NEAR)


def far(value):
    return lax.ppermute(value, "y", FAR)


def swap(value):
    return lax.ppermute(value, "core", SWAP)


def up(value):
    return lax.ppermute(value, "z", [(place, (place + 1) % 8) for place in range(8)])


def down(value):
    return lax.ppermute(value, "z", [(place, (place - 1) % 8) for place in range(8)])


def beside(value):
    return lax.ppermute(value, "pipe", NEAR)


def around(value):
    return lax.ppermute(value, "pipe", FAR)


SHALLOW = (256, 0, 128, 256)
OFFSETS = (0, 7, 6, 5, 1, 2, 3, 4)


def block_kernel(ctl, *refs, tokens, shallow, pieces):
    mine, by_near, by_far, cross, swapped, swapped_cross = refs[:6]
    weights = refs[6 : 6 + pieces]
    keep, give, held, normed, sums, mixed_all, sems = refs[6 + pieces :]
    size = sums.shape[2]
    copies = []
    for index in range(4):
        pairs = []
        if shallow:
            rows = pl.ds(0, shallow)
            pairs += [(weights[slot].at[index], held.at[index, slot, rows]) for slot in range(7)]
            pairs.append((weights[7 + index // 2].at[index % 2], held.at[index, 7, rows]))
        if shallow < size:
            rows = pl.ds(shallow, size - shallow)
            base = 2 * index + (9 if shallow else 0)
            pairs += [
                (weights[base + half], held.at[index, pl.ds(4 * half, 4), rows]) for half in range(2)
            ]
        copies.append(
            [
                pltpu.make_async_copy(source, place, sems.at[index, number])
                for number, (source, place) in enumerate(pairs)
            ]
        )
    for group in copies:
        for copy in group:
            copy.start()
    flip, core, section, depth = ctl[0], ctl[1], ctl[4], ctl[5]

    def columns(slot):
        place = (depth + ctl[8 + slot]) & 7
        return pl.ds(pl.multiple_of(place * size, 128), size)

    @pl.loop(0, 8)
    def _(slot):
        cols, to = columns(slot), pl.ds(pl.multiple_of(slot * size, 128), size)
        for block, (own, other) in enumerate(
            ((mine, swapped.at[0]), (by_near, swapped.at[1]), (cross, swapped_cross), (by_far, swapped.at[2]))
        ):
            normed[pl.ds(2 * block * tokens, tokens), to] = own[:, cols]
            normed[pl.ds((2 * block + 1) * tokens, tokens), to] = other[:, cols]

    @pl.loop(0, 4)
    def _(index):
        array = section ^ index
        for number, group in enumerate(copies):

            @pl.when(index == number)
            def _():
                for copy in group:
                    copy.wait()

        @pl.when(array != 3)
        def _():
            sums[array] = jnp.dot(
                normed[...],
                held[index].reshape(8 * size, size),
                preferred_element_type=jnp.float32,
            )

    rows = 4 * tokens
    heads = size // HEAD
    key_place = lax.broadcasted_iota(jnp.int32, (rows, rows), 1) ^ flip
    query_place = lax.broadcasted_iota(jnp.int32, (rows, HEAD), 0) ^ flip
    video = 3 * tokens
    first = jnp.where(core == 0, video, 0)
    own_low = jnp.where(core == 0, 0, video)
    own_high = jnp.where(core == 0, video, rows)
    live = (query_place >= own_low) & (query_place < own_high)
    for sample in range(2):
        valid = (key_place >= first) & (key_place < first + ctl[2 + sample])
        span = pl.ds(sample * rows, rows)
        spans = [pl.ds(head * HEAD, HEAD) for head in range(heads)]
        scores = [
            lax.dot_general(
                (sums[0, span, cols] * HEAD ** (-0.5)).astype(jnp.bfloat16),
                sums[1, span, cols].astype(jnp.bfloat16),
                (((1,), (1,)), ((), ())),
                preferred_element_type=jnp.float32,
            )
            for cols in spans
        ]
        scores = [jnp.where(valid, score, -1e30) for score in scores]
        powers = [jnp.exp(score - jnp.max(score, axis=-1, keepdims=True)) for score in scores]
        shares = [
            (power * (1.0 / jnp.sum(power, axis=-1, keepdims=True))).astype(jnp.bfloat16)
            for power in powers
        ]
        mixed = [
            jnp.dot(share, sums[2, span, cols].astype(jnp.bfloat16), preferred_element_type=jnp.float32)
            for share, cols in zip(shares, spans)
        ]
        for head, cols in enumerate(spans):
            mixed_all[span, cols] = jnp.where(live, mixed[head], 0.0).astype(jnp.bfloat16)
    last = section ^ 3

    def project(piece, slot):
        made = lax.dot_general(
            mixed_all[...], piece, (((1,), (1,)), ((), ())), preferred_element_type=jnp.float32
        ).astype(jnp.bfloat16)
        for block in range(4):
            keep[block, :, columns(slot)] = made[2 * block * tokens : (2 * block + 1) * tokens]
            give[block, :, columns(slot)] = made[(2 * block + 1) * tokens : (2 * block + 2) * tokens]

    @pl.loop(0, 8)
    def _(slot):
        project(held[last, slot], slot)


def run_block(ctl, blocks, weights, tokens, width, shallow):
    size = weights[0].shape[2]
    vmem = pl.BlockSpec(memory_space=pltpu.VMEM)
    out = jax.ShapeDtypeStruct((4, tokens, width), jnp.bfloat16)
    count = 8 * tokens
    there = pl.BlockSpec(memory_space=pltpu.HBM)
    return pl.pallas_call(
        functools.partial(
            block_kernel, tokens=tokens, shallow=shallow, pieces=len(weights)
        ),
        out_shape=(out, out),
        in_specs=[pl.BlockSpec(memory_space=pltpu.SMEM)] + [vmem] * 6 + [there] * len(weights),
        out_specs=(vmem, vmem),
        scratch_shapes=[
            pltpu.VMEM((4, 8, size, size), jnp.bfloat16),
            pltpu.VMEM((count, width), jnp.bfloat16),
            pltpu.VMEM((3, count, size), jnp.float32),
            pltpu.VMEM((count, size), jnp.bfloat16),
            pltpu.SemaphoreType.DMA((4, 10)),
        ],
        compiler_params=pltpu.CompilerParams(vmem_limit_bytes=24 << 20),
        cost_estimate=pl.CostEstimate(
            flops=8 * count * width * size,
            bytes_accessed=8 * width * size + 6 * count * width,
            transcendentals=count * size,
        ),
    )(ctl, *blocks, *weights)


def pack_kernel(query, key, value, out, packed):
    quarter = packed.shape[4]
    for tower in range(2):
        for part in range(4):
            cols = pl.ds(part * quarter, quarter)
            packed[0, part, tower] = query[tower, :, cols]
            packed[1, part, tower] = key[tower, :, cols]
            packed[2, part, tower] = value[tower, :, cols]
            packed[3, part, tower] = out[tower, cols, :].T


def pack(query, key, value, out):
    towers, rows, features = query.shape
    vmem = pl.BlockSpec(memory_space=pltpu.VMEM)
    return pl.pallas_call(
        pack_kernel,
        out_shape=jax.ShapeDtypeStruct((4, 4, towers, rows, features // 4), jnp.bfloat16),
        in_specs=[vmem] * 4,
        out_specs=vmem,
    )(query, key, value, out)


def gather_tokens(mine):
    half = mine.shape[0] // 2
    by_near, by_far = near(mine), far(mine)
    pair = swap(jnp.stack([mine, by_near, by_far]))
    cross = jnp.concatenate([near(by_far[:half]), far(by_near[half:])])
    return mine, by_near, by_far, cross, pair, swap(cross)


def reduce_tokens(state, keep, give):
    half = state.shape[0] // 2
    total = keep + swap(give)
    low = near(total[2, :half]).astype(jnp.float32)
    high = far(total[2, half:]).astype(jnp.float32)
    to_far = jnp.concatenate(
        [(total[3, :half].astype(jnp.float32) + low).astype(jnp.bfloat16), total[3, half:]]
    )
    to_near = jnp.concatenate(
        [total[1, :half], (total[1, half:].astype(jnp.float32) + high).astype(jnp.bfloat16)]
    )
    by_near, by_far = near(to_near), far(to_far)
    update = total[0].astype(jnp.float32) + by_near.astype(jnp.float32) + by_far.astype(jnp.float32)
    return (state.astype(jnp.float32) + update).astype(jnp.bfloat16)


def across(shard):
    by_beside, by_around = beside(shard), around(shard)
    return jnp.stack([shard, by_beside, beside(by_around), by_around])


def deep(block):
    below = [up(block)]
    above = [down(block)]
    for _ in range(2):
        below.append(up(below[-1]))
        above.append(down(above[-1]))
    return below, above


def finish_deep(four):
    below, above = deep(four)
    return [four, *below, *above, up(below[-1][:2]), down(above[-1][2:])]


def finish_across(lower, upper):
    by_beside = beside(lower), beside(upper)
    by_around = around(lower), around(upper)
    crossed = beside(by_around[0]), around(by_beside[1])
    return [lower, upper, *by_beside, *crossed, *by_around]


def spread(shards):
    zero, one, two, three = shards
    cut = SHALLOW
    size = zero.shape[0]
    shallow = [finish_deep(across(zero[: cut[0]])), []]
    both = across(jnp.concatenate([two[: cut[2]], three[: cut[3]]]))
    shallow.append(finish_deep(both[:, : cut[2]]))
    shallow.append(finish_deep(both[:, cut[2] :]))
    rest = zero[cut[0] :]
    below, above = deep(rest)
    lower = jnp.stack([rest, *below])
    upper = jnp.stack([*above, up(below[-1])])
    across_all = [finish_across(lower, upper)]
    rest = jnp.concatenate([one, two[cut[2] :], three[cut[3] :]])
    below, above = deep(rest)
    ends = up(below[-1][:size]), down(above[-1][size:])
    start = 0
    for layer in (1, 2, 3):
        stop = start + size - cut[layer]
        end = ends[0] if layer == 1 else ends[1][start - size : stop - size]
        lower = jnp.stack([part[start:stop] for part in [rest, *below]])
        upper = jnp.stack([part[start:stop] for part in above] + [end])
        across_all.append(finish_across(lower, upper))
        start = stop
    return [early + late for early, late in zip(shallow, across_all)]


def section(hidden, w_query, w_key, w_value, w_out, video_len, audio_len):
    batch = lax.axis_index("pipe")
    depth = lax.axis_index("z")
    ring = lax.axis_index("y")
    core = lax.axis_index("core")
    _, tokens, width = hidden.shape
    features = w_query.shape[3]
    rows = w_query.shape[2]
    quarter = features // 4
    layers = 4
    parts = pack(w_query[0], w_key[0], w_value[0], w_out[0]).reshape(32, rows, quarter)
    moved = lax.all_to_all(parts, ("pipe", "y", "core"), 0, 0, tiled=True)
    moved = moved.reshape(layers, 8 * rows, quarter)
    gathered = spread(moved)
    state = lax.dynamic_index_in_dim(hidden, batch, 0, keepdims=False)
    low, high = ring % 2, ring // 2
    lengths = jnp.where(core == 0, audio_len[batch], video_len[batch])
    flip = 2 * tokens * low + tokens * core
    zero = jnp.int32(0)
    ctl = jnp.stack(
        [flip, core, lengths[2 * depth + high], lengths[2 * depth + 1 - high], batch, depth, zero, zero]
        + [jnp.int32(offset) for offset in OFFSETS]
    ).astype(jnp.int32)
    for layer in range(layers):
        blocks = gather_tokens(rms_norm(state))
        keep, give = run_block(ctl, blocks, gathered[layer], tokens, width, SHALLOW[layer])
        state = reduce_tokens(state, keep, give)
    return state[None]


def solution(mesh):
    inner = Mesh(mesh.devices.reshape(4, 8, 4, 2), ("pipe", "z", "y", "core"))
    dp = ("z", "y", "core")
    return jax.shard_map(
        section,
        mesh=inner,
        in_specs=(
            P(None, dp, None),
            P("pipe", None, dp, None),
            P("pipe", None, dp, None),
            P("pipe", None, dp, None),
            P("pipe", None, None, dp),
            P(),
            P(),
        ),
        out_specs=P("pipe", dp, None),
        check_vma=False,
    )
```
